32 devices in a mesh: grp: 2 (over y), row: 4 (over z), col: 2 (over x), half: 2 (over core).
Axes of the slice: x: 2, y: 2, z: 4, core: 2. Of those that a mesh axis runs over, the one named last changes fastest.
Arguments:
- vecs: bfloat16 [4, 1024, 32768], P(('grp', 'half'), 'row', 'col'), parts along dimension 0, may hold values from -6 to 6
- poles: float32 [4, 32768], P(('grp', 'half'), 'col'), parts along dimension 0, may hold values from -512 to 512, as said below
- weights: float32 [4, 32768], P(('grp', 'half'), 'col'), parts along dimension 0, may hold values from -5 to 5
- kept: int32 [4, 32768], P(('grp', 'half'), 'col'), parts along dimension 0, may hold values 0 or 1
- roots: float32 [1024], P(('grp', 'row')), parts along dimension 0, may hold values from -512 to 512, as said below
- order: int32 [1024], P('grp'), parts along dimension 0, may hold values from 0 to 511, each once
Outputs:
- merged: bfloat16 [16, 4, 2, 32, 512], P(('grp', 'row', 'half'), None, None, None, 'col'), parts along dimension 0
The draws below stay inside these ranges and needn't reach their ends.
There are 2 independent parts, one for each index of `grp`. The reference program is written for one: setup_inputs(seed, part) draws one part's arguments, and reference() takes and returns one part's arrays. A program takes and returns all parts, laid end to end along the dimension named above; each array names one. Nothing has to cross between parts.
Inputs may be any that keep to these rules, and one draw needn't show every extreme that they name: `poles`: every root differs from every pole by 0.2 or more. `roots`: every root differs from every pole by 0.2 or more. `order`: A permutation of 0 to 511.
All inputs are finite; a program needn't handle non-finite values. No bound on the sum of `kept` on one device may be relied on, other than what follows from the above.
Results may differ from the reference program's by a relative error of at most 0.0049.
Values may be sent and summed in bfloat16 or wider, within the bound.
A program may use at most 64 MiB of HBM per device.

```python
import jax
import jax.numpy as jnp
from jax import lax

NH = 32768
PANEL = 512
BINS = 1024
QROWS = 1024
BS = 32
N_ROW = 4


def draw_poles(key, part):
    first = jax.random.fold_in(key, 11)
    second = jax.random.fold_in(key, 12)
    levels = jax.random.randint(first, (2, NH), -(BINS // 2), BINS // 2)
    frac = jax.random.uniform(second, (2, NH), jnp.float32, 0.0, 0.3)
    return levels.astype(jnp.float32) + frac


def draw_roots(key, part):
    first = jax.random.fold_in(key, 21)
    second = jax.random.fold_in(key, 22)
    levels = jax.random.randint(first, (PANEL,), -(BINS // 2), BINS // 2 - 1)
    frac = jax.random.uniform(second, (PANEL,), jnp.float32, 0.5, 0.8)
    return levels.astype(jnp.float32) + frac


def place_ends(drawn, stream_key, least, largest):
    extent = drawn.shape
    place = [jax.random.randint(jax.random.fold_in(stream_key, axis), (), 0, extent[axis]) for axis in range(len(extent))]
    drawn = drawn.at[tuple(place)].set(least)
    longest = extent.index(max(extent))
    place[longest] = (place[longest] + 1) % extent[longest]
    return drawn.at[tuple(place)].set(largest)


def shard_levels(key, extent, split, smallest, largest):
    loudness = 1.0
    for dim, blocks in split:
        draws = jax.random.uniform(jax.random.fold_in(jax.random.fold_in(key, 6), dim), (blocks,), jnp.float32, smallest / len(split), largest / len(split))
        loudness = loudness * jnp.repeat(jnp.exp(draws), extent[dim] // blocks).reshape((-1,) + (1,) * (len(extent) - 1 - dim))
    return loudness


def bell_draw(stream_key, dims, width, limit, shards=(), dtype=jnp.bfloat16):
    level = shard_levels(stream_key, dims, shards, -0.22, 0.18) if shards else 1.0
    drawn = jax.random.normal(stream_key, dims, jnp.float32) * width * level
    return jnp.minimum(jnp.maximum(drawn, -limit), limit).astype(dtype)


def setup_inputs(seed: int = 0, part: int = 0) -> dict:
    keys = jax.random.split(jax.random.key(seed), 7)
    part_splits = jax.random.split(jax.random.fold_in(keys[6], part), 7)
    return {
        "vecs": bell_draw(part_splits[0], (2, QROWS, NH), 1.0, 6.0, ((0, 2), (1, 4), (2, 2))),
        "poles": draw_poles(jax.random.fold_in(jax.random.fold_in(keys[6], part), 71), part),
        "weights": bell_draw(part_splits[2], (2, NH), 1.0, 5.0, ((0, 2), (1, 2)), jnp.float32),
        "kept": place_ends((jax.random.randint(part_splits[3], (2, NH), 0, 4) < 3).astype(jnp.int32), jax.random.fold_in(part_splits[3], 1), 0, 1),
        "roots": draw_roots(jax.random.fold_in(jax.random.fold_in(keys[6], part), 71), part),
        "order": jax.random.permutation(part_splits[5], PANEL).astype(jnp.int32),
    }


def reference(vecs, poles, weights, kept, roots, order):
    theta = roots[order.astype(jnp.int32)]
    scaled = weights * kept.astype(jnp.float32)
    cauchy = scaled[:, :, None] / (poles[:, :, None] - theta[None, None, :])
    norms = lax.optimization_barrier(jnp.sum(cauchy * cauchy, axis=(0, 1)))
    zpanel = (cauchy * lax.rsqrt(norms + 1e-06)).astype(jnp.bfloat16)
    upper = jnp.dot(vecs[0], zpanel[0], preferred_element_type=jnp.float32).astype(jnp.bfloat16)
    lower = jnp.dot(vecs[1], zpanel[1], preferred_element_type=jnp.float32).astype(jnp.bfloat16)
    product = jnp.stack([upper, lower], axis=0)
    blocks = product.reshape(2, N_ROW, 2 * N_ROW, BS, PANEL)
    return jnp.transpose(blocks, (2, 1, 0, 3, 4))
```

```python
import functools

import jax
import jax.numpy as jnp
from jax import lax
from jax.experimental import pallas as pl
from jax.experimental.pallas import tpu as pltpu
from jax.sharding import PartitionSpec as P

MESH = pl.DeviceIdType.MESH
LANES = 128
PAIRED = 0


def kernel(dims, vecs, poles, weights, kept, roots, order, out,
           vbuf, rootbuf, theta, scaled, picks, raw, mask, centers, own, zeven, zodd, acc, nacc, asend, arecv,
           nsend, nrecv, fsend, frecv,
           ssem, vsem, rsend, rrecv, nssem, nrsem, fssem, frsem, assem, arsem):
    n_row, n_col, n_half, cols, panel, slab = dims
    grp, row, col, half = (lax.axis_index(a) for a in ("grp", "row", "col", "half"))
    share = panel // n_col
    width = panel // n_row
    nrows = vbuf.shape[1]
    groups = n_row * n_half
    depth = nrows // groups
    n_slabs = cols // slab
    tiles = slab // LANES
    me = row * n_half + half

    barrier = pltpu.get_barrier_semaphore()
    for o in range(1, groups):
        g = lax.rem(me + o, groups)
        pl.semaphore_signal(barrier, inc=1, device_id=(grp, g // n_half, col, lax.rem(g, n_half)), device_id_type=MESH)
    for t in range(1, n_col):
        for h in range(n_half):
            pl.semaphore_signal(barrier, inc=1, device_id=(grp, row, lax.rem(col + t, n_col), h), device_id_type=MESH)

    small = [(roots, own), (weights, raw), (kept, mask), (poles, centers), (order, picks)]
    fetches = [pltpu.make_async_copy(src, dst, ssem.at[n]) for n, (src, dst) in enumerate(small)]
    for fetch in fetches:
        fetch.start()

    def fetch_tile(n, carry):
        at = pl.ds(pl.multiple_of(n * LANES, LANES), LANES)
        pltpu.make_async_copy(vecs.at[0, :, at], vbuf.at[n], vsem.at[n // tiles]).start()
        return carry

    def loaded(i):
        here = vbuf.at[pl.ds(i * tiles, tiles)]
        pltpu.make_async_copy(here, here, vsem.at[i]).wait()

    lax.fori_loop(0, n_slabs * tiles, fetch_tile, 0)
    acc[...] = jnp.zeros_like(acc)
    zodd[...] = jnp.zeros_like(zodd)
    pl.semaphore_wait(barrier, groups - 1 + (n_col - 1) * n_half)

    def root_copy(o, h):
        return pltpu.make_async_remote_copy(
            src_ref=roots, dst_ref=rootbuf.at[o], send_sem=rsend.at[o, h], recv_sem=rrecv.at[o],
            device_id=(grp, lax.rem(row + o, n_row), col, h), device_id_type=MESH)

    @pl.when(half == n_half - 1)
    def _():
        for o in range(1, n_row):
            for h in range(n_half):
                root_copy(o, h).start()

    for fetch in fetches:
        fetch.wait()
    scaled[...] = raw[...] * mask[...].astype(jnp.float32)
    nacc[...] = jnp.zeros_like(nacc)
    span = min(width, 128)

    for first in range(0, width, span):
        mine = [jnp.transpose(jnp.broadcast_to(own[:, first:first + span], (LANES, span)))[r:r + 8] for r in range(0, span, 8)]

        def norm_step(i, squares):
            for j in range(4):
                at = pl.ds(pl.multiple_of(i * 4 * LANES + j * LANES, LANES), LANES)
                weight, center = scaled[:, at], centers[:, at]
                cauchy = [weight / (center - m) for m in mine]
                squares = [s + c * c for s, c in zip(squares, cauchy)]
            return squares

        squares = lax.fori_loop(0, cols // (4 * LANES), norm_step, [jnp.zeros((8, LANES), jnp.float32) for _ in mine])
        for n, s in enumerate(squares):
            nacc[pl.ds(first + n * 8, 8), :] = s
    nsend[...] = jnp.sum(jnp.transpose(nacc[...]), axis=0, keepdims=True)

    def norm_copy(t, o):
        return pltpu.make_async_remote_copy(
            src_ref=nsend, dst_ref=nrecv.at[t, o], send_sem=nssem.at[t, o], recv_sem=nrsem.at[t, o],
            device_id=(grp, row, lax.rem(col + t, n_col), lax.rem(half + o, n_half)), device_id_type=MESH)

    norm_copies = [(t, o) for t in range(n_col) for o in range(n_half) if t or o]
    for t, o in norm_copies:
        norm_copy(t, o).start()

    wanted = jnp.transpose(jnp.broadcast_to(picks[...], (LANES, panel)))[:, :width]
    lane = lax.broadcasted_iota(jnp.int32, (panel, width), 1)
    picked = jnp.zeros((panel, width), jnp.float32)
    for o in range(n_row):
        if o:
            root_copy(o, 0).wait_recv()
        source = lax.rem(row + n_row - o, n_row)
        picked = jnp.where(wanted - source * width == lane, rootbuf[o] if o else own[...], picked)
    theta[...] = jnp.broadcast_to(jnp.sum(picked, axis=1, keepdims=True), (panel, LANES))

    def dot(z, i, k):
        acc[...] += lax.dot_general(
            jnp.concatenate([vbuf[(i * 2 + k) * tiles + j] for j in range(tiles)], axis=1),
            jnp.concatenate([z[k * tiles + j] for j in range(tiles)], axis=1),
            (((1,), (1,)), ((), ())), preferred_element_type=jnp.float32)

    def piece_copy(t, o):
        g = lax.rem(me + o, groups)
        return pltpu.make_async_remote_copy(
            src_ref=asend.at[t, g], dst_ref=arecv.at[t, o], send_sem=assem.at[t, o], recv_sem=arsem.at[t, o],
            device_id=(grp, g // n_half, lax.rem(col + t, n_col), lax.rem(g, n_half)), device_id_type=MESH)

    def flush(t):
        asend[t] = acc[...].reshape(groups, depth, share).astype(jnp.bfloat16)
        for o in range(0 if t else 1, groups):
            piece_copy(t, o).start()

    def chunk(t, last):
        base = lax.rem(col + t, n_col) * share

        def fill(z, i, k):
            thetas = [theta[pl.ds(pl.multiple_of(base + r, 16), 16), :] for r in range(0, share, 16)]
            for j in range(tiles):
                at = pl.ds(pl.multiple_of((i * 2 + k) * slab + j * LANES, LANES), LANES)
                weight, center = scaled[:, at], centers[:, at]
                for n in range(0, share // 16, 2):
                    a, b = (center - th for th in thetas[n:n + 2])
                    if (n // 2) % 4 < PAIRED:
                        both = weight / (a * b)
                        left, right = both * b, both * a
                    else:
                        left, right = weight / a, weight / b
                    z[k * tiles + j, pl.ds(n * 16, 16), :] = left.astype(jnp.bfloat16)
                    z[k * tiles + j, pl.ds(n * 16 + 16, 16), :] = right.astype(jnp.bfloat16)

        def pair(p, carry):
            if last is None:
                for n in range(4):
                    loaded(4 * p + n)
            before = jnp.where(p == 0, 0 if last is None else n_slabs // 2 - 1, 2 * p - 1)

            def even(k, carry):
                dot(zodd, before, k)
                fill(zeven, 2 * p, k)
                return carry

            def odd(k, carry):
                dot(zeven, 2 * p, k)
                fill(zodd, 2 * p + 1, k)
                return carry

            lax.fori_loop(0, 2, even, 0)

            @pl.when(p == 0)
            def _():
                if last is not None:
                    flush(last)
                acc[...] = jnp.zeros_like(acc)

            lax.fori_loop(0, 2, odd, 0)
            return carry

        lax.fori_loop(0, n_slabs // 4, pair, 0)

    last = None
    for t in [*range(1, n_col), 0]:
        chunk(t, last)
        if last is None:
            total = nsend[...]
            for pair in norm_copies:
                norm_copy(*pair).wait()
                total += nrecv[pair]
            fsend[...] = lax.rsqrt(total + 1e-06)

            def factor_copy(o):
                return pltpu.make_async_remote_copy(
                    src_ref=fsend, dst_ref=frecv.at[o], send_sem=fssem.at[o], recv_sem=frsem.at[o],
                    device_id=(grp, lax.rem(row + o, n_row), col, half), device_id_type=MESH)

            for o in range(1, n_row):
                factor_copy(o).start()
        last = t

    def rest(k, carry):
        dot(zodd, n_slabs // 2 - 1, k)
        return carry

    lax.fori_loop(0, 2, rest, 0)
    flush(0)

    chosen = picks[:, pl.ds(pl.multiple_of(col * share, LANES), share)]
    index = lax.broadcasted_iota(jnp.int32, (width, share), 0)
    scale = jnp.zeros((width, share), jnp.float32)
    for o in range(n_row):
        if o:
            factor_copy(o).wait()
        source = lax.rem(row + n_row - o, n_row)
        factor = frecv[o] if o else fsend[...]
        column = jnp.transpose(jnp.broadcast_to(factor, (LANES, width)))[:, :1]
        scale = jnp.where(chosen - source * width == index, column, scale)
    scale = jnp.sum(scale, axis=0, keepdims=True)

    @pl.when(half == n_half - 1)
    def _():
        for o in range(1, n_row):
            for h in range(n_half):
                root_copy(o, h).wait_send()

    for o in range(groups):
        g = lax.rem(me + groups - o, groups)
        piece = jnp.zeros((depth, share), jnp.float32)
        for t in [*range(1, n_col), 0]:
            if t or o:
                piece_copy(t, o).wait()
            piece += (arecv[t, o] if t or o else asend[0, me]).astype(jnp.float32)
        out[0, g // n_half, lax.rem(g, n_half)] = (piece * scale).astype(jnp.bfloat16)


def body(vecs, poles, weights, kept, roots, order):
    n_row, n_col, n_half = (lax.axis_size(a) for a in ("row", "col", "half"))
    nrows, cols = vecs.shape[1:]
    panel = order.shape[0]
    share, groups, width = panel // n_col, n_row * n_half, panel // n_row
    depth = nrows // groups
    slab = min(2048, cols // 4)
    dma = pltpu.SemaphoreType.DMA
    return pl.pallas_call(
        functools.partial(kernel, (n_row, n_col, n_half, cols, panel, slab)),
        out_shape=pltpu.VMEM((1, n_row, n_half, depth, share), jnp.bfloat16),
        in_specs=[pl.BlockSpec(memory_space=pl.ANY)] * 6,
        out_specs=pl.BlockSpec(memory_space=pltpu.VMEM),
        scratch_shapes=[
            pltpu.VMEM((cols // LANES, nrows, LANES), jnp.bfloat16),
            pltpu.VMEM((n_row, 1, width), jnp.float32),
            pltpu.VMEM((panel, LANES), jnp.float32),
            pltpu.VMEM((1, cols), jnp.float32),
            pltpu.VMEM((1, panel), jnp.int32),
            pltpu.VMEM((1, cols), jnp.float32),
            pltpu.VMEM((1, cols), jnp.int32),
            pltpu.VMEM((1, cols), jnp.float32),
            pltpu.VMEM((1, width), jnp.float32),
            pltpu.VMEM((2 * slab // LANES, share, LANES), jnp.bfloat16),
            pltpu.VMEM((2 * slab // LANES, share, LANES), jnp.bfloat16),
            pltpu.VMEM((nrows, share), jnp.float32),
            pltpu.VMEM((width, LANES), jnp.float32),
            pltpu.VMEM((n_col, groups, depth, share), jnp.bfloat16),
            pltpu.VMEM((n_col, groups, depth, share), jnp.bfloat16),
            pltpu.VMEM((1, width), jnp.float32),
            pltpu.VMEM((n_col, n_half, 1, width), jnp.float32),
            pltpu.VMEM((1, width), jnp.float32),
            pltpu.VMEM((n_row, 1, width), jnp.float32),
            dma((5,)),
            dma((cols // slab,)),
            dma((n_row, n_half)),
            dma((n_row,)),
            dma((n_col, n_half)),
            dma((n_col, n_half)),
            dma((n_row,)),
            dma((n_row,)),
            dma((n_col, groups)),
            dma((n_col, groups)),
        ],
        compiler_params=pltpu.CompilerParams(collective_id=0, has_side_effects=True),
        name="merge",
    )(vecs, poles, weights, kept, roots[None, :], order[None, :])


def solution(mesh):
    return jax.shard_map(
        body,
        mesh=mesh,
        in_specs=(
            P(("grp", "half"), "row", "col"),
            P(("grp", "half"), "col"),
            P(("grp", "half"), "col"),
            P(("grp", "half"), "col"),
            P(("grp", "row")),
            P("grp"),
        ),
        out_specs=P(("grp", "row", "half"), None, None, None, "col"),
        check_vma=False,
    )
```

```python
import functools

import jax
import jax.numpy as jnp
from jax import lax
from jax.experimental import pallas as pl
from jax.experimental.pallas import tpu as pltpu
from jax.sharding import PartitionSpec as P

MESH = pl.DeviceIdType.MESH
LANES = 128
PAIRED = 1
SLAB = 8192


def kernel(dims, vecs, poles, weights, kept, roots, order, out,
           vbuf, rootbuf, theta, scaled, picks, raw, mask, centers, own, z, acc, nacc, asend, arecv,
           nsend, nrecv, fsend, frecv,
           ssem, vsem, rsend, rrecv, nssem, nrsem, fssem, frsem, assem, arsem):
    n_row, n_col, n_half, cols, panel, slab = dims
    grp, row, col, half = (lax.axis_index(a) for a in ("grp", "row", "col", "half"))
    share = panel // n_col
    width = panel // n_row
    nrows = vbuf.shape[1]
    groups = n_row * n_half
    depth = nrows // groups
    n_slabs = cols // slab
    tiles = slab // LANES
    me = row * n_half + half

    barrier = pltpu.get_barrier_semaphore()
    for o in range(1, groups):
        g = lax.rem(me + o, groups)
        pl.semaphore_signal(barrier, inc=1, device_id=(grp, g // n_half, col, lax.rem(g, n_half)), device_id_type=MESH)
    for t in range(1, n_col):
        for h in range(n_half):
            pl.semaphore_signal(barrier, inc=1, device_id=(grp, row, lax.rem(col + t, n_col), h), device_id_type=MESH)

    small = [(roots, own), (weights, raw), (kept, mask), (poles, centers), (order, picks)]
    fetches = [pltpu.make_async_copy(src, dst, ssem.at[n]) for n, (src, dst) in enumerate(small)]
    for fetch in fetches:
        fetch.start()

    def fetch_tile(n, carry):
        at = pl.ds(pl.multiple_of(n * LANES, LANES), LANES)
        pltpu.make_async_copy(vecs.at[0, :, at], vbuf.at[n], vsem.at[n // tiles]).start()
        return carry

    def loaded(i):
        here = vbuf.at[pl.ds(i * tiles, tiles)]
        pltpu.make_async_copy(here, here, vsem.at[i]).wait()

    lax.fori_loop(0, n_slabs * tiles, fetch_tile, 0)
    pl.semaphore_wait(barrier, groups - 1 + (n_col - 1) * n_half)

    def root_copy(o, h):
        return pltpu.make_async_remote_copy(
            src_ref=roots, dst_ref=rootbuf.at[o], send_sem=rsend.at[o, h], recv_sem=rrecv.at[o],
            device_id=(grp, lax.rem(row + o, n_row), col, h), device_id_type=MESH)

    @pl.when(half == n_half - 1)
    def _():
        for o in range(1, n_row):
            for h in range(n_half):
                root_copy(o, h).start()

    for fetch in fetches:
        fetch.wait()
    scaled[...] = raw[...] * mask[...].astype(jnp.float32)
    nacc[...] = jnp.zeros_like(nacc)
    span = min(width, 128)

    for first in range(0, width, span):
        mine = [jnp.transpose(jnp.broadcast_to(own[:, first:first + span], (LANES, span)))[r:r + 8] for r in range(0, span, 8)]

        def norm_step(i, squares):
            for j in range(4):
                at = pl.ds(pl.multiple_of(i * 4 * LANES + j * LANES, LANES), LANES)
                weight, center = scaled[:, at], centers[:, at]
                cauchy = [weight / (center - m) for m in mine]
                squares = [s + c * c for s, c in zip(squares, cauchy)]
            return squares

        squares = lax.fori_loop(0, cols // (4 * LANES), norm_step, [jnp.zeros((8, LANES), jnp.float32) for _ in mine])
        for n, s in enumerate(squares):
            nacc[pl.ds(first + n * 8, 8), :] = s
    nsend[...] = jnp.sum(jnp.transpose(nacc[...]), axis=0, keepdims=True)

    def norm_copy(t, o):
        return pltpu.make_async_remote_copy(
            src_ref=nsend, dst_ref=nrecv.at[t, o], send_sem=nssem.at[t, o], recv_sem=nrsem.at[t, o],
            device_id=(grp, row, lax.rem(col + t, n_col), lax.rem(half + o, n_half)), device_id_type=MESH)

    norm_copies = [(t, o) for t in range(n_col) for o in range(n_half) if t or o]
    for t, o in norm_copies:
        norm_copy(t, o).start()

    wanted = jnp.transpose(jnp.broadcast_to(picks[...], (LANES, panel)))[:, :width]
    lane = lax.broadcasted_iota(jnp.int32, (panel, width), 1)
    picked = jnp.zeros((panel, width), jnp.float32)
    for o in range(n_row):
        if o:
            root_copy(o, 0).wait_recv()
        source = lax.rem(row + n_row - o, n_row)
        picked = jnp.where(wanted - source * width == lane, rootbuf[o] if o else own[...], picked)
    theta[...] = jnp.broadcast_to(jnp.sum(picked, axis=1, keepdims=True), (panel, LANES))

    def piece_copy(t, o):
        g = lax.rem(me + o, groups)
        return pltpu.make_async_remote_copy(
            src_ref=asend.at[t, g], dst_ref=arecv.at[t, o], send_sem=assem.at[t, o], recv_sem=arsem.at[t, o],
            device_id=(grp, g // n_half, lax.rem(col + t, n_col), lax.rem(g, n_half)), device_id_type=MESH)

    def flush(t):
        asend[t] = acc[...].reshape(groups, depth, share).astype(jnp.bfloat16)
        for o in range(0 if t else 1, groups):
            piece_copy(t, o).start()

    def chunk(t):
        base = lax.rem(col + t, n_col) * share
        acc[...] = jnp.zeros_like(acc)

        def step(i, carry):
            if t == 1 or n_col == 1:
                loaded(i)
            thetas = [theta[pl.ds(pl.multiple_of(base + r, 16), 16), :] for r in range(0, share, 16)]
            sums = [None, None]
            for m in range(tiles // 2):
                for j in (2 * m, 2 * m + 1):
                    at = pl.ds(pl.multiple_of(i * slab + j * LANES, LANES), LANES)
                    weight, center = scaled[:, at], centers[:, at]
                    for n in range(0, share // 16, 2):
                        a, b = (center - th for th in thetas[n:n + 2])
                        if (n // 2) % 4 < PAIRED:
                            both = weight / (a * b)
                            left, right = both * b, both * a
                        else:
                            left, right = weight / a, weight / b
                        z[j, pl.ds(n * 16, 16), :] = left.astype(jnp.bfloat16)
                        z[j, pl.ds(n * 16 + 16, 16), :] = right.astype(jnp.bfloat16)
                part = lax.dot_general(
                    jnp.concatenate([vbuf[i * tiles + j] for j in (2 * m, 2 * m + 1)], axis=1),
                    jnp.concatenate([z[j] for j in (2 * m, 2 * m + 1)], axis=1),
                    (((1,), (1,)), ((), ())), preferred_element_type=jnp.float32)
                sums[m % 2] = part if sums[m % 2] is None else sums[m % 2] + part
            acc[...] += sums[0] + sums[1]
            return carry

        lax.fori_loop(0, n_slabs, step, 0)

    for t in [*range(1, n_col), 0]:
        chunk(t)
        flush(t)
        if t == 1 or n_col == 1:
            total = nsend[...]
            for pair in norm_copies:
                norm_copy(*pair).wait()
                total += nrecv[pair]
            fsend[...] = lax.rsqrt(total + 1e-06)

            def factor_copy(o):
                return pltpu.make_async_remote_copy(
                    src_ref=fsend, dst_ref=frecv.at[o], send_sem=fssem.at[o], recv_sem=frsem.at[o],
                    device_id=(grp, lax.rem(row + o, n_row), col, half), device_id_type=MESH)

            for o in range(1, n_row):
                factor_copy(o).start()

    chosen = picks[:, pl.ds(pl.multiple_of(col * share, LANES), share)]
    index = lax.broadcasted_iota(jnp.int32, (width, share), 0)
    scale = jnp.zeros((width, share), jnp.float32)
    for o in range(n_row):
        if o:
            factor_copy(o).wait()
        source = lax.rem(row + n_row - o, n_row)
        factor = frecv[o] if o else fsend[...]
        column = jnp.transpose(jnp.broadcast_to(factor, (LANES, width)))[:, :1]
        scale = jnp.where(chosen - source * width == index, column, scale)
    scale = jnp.sum(scale, axis=0, keepdims=True)

    @pl.when(half == n_half - 1)
    def _():
        for o in range(1, n_row):
            for h in range(n_half):
                root_copy(o, h).wait_send()

    for o in range(groups):
        g = lax.rem(me + groups - o, groups)
        piece = jnp.zeros((depth, share), jnp.float32)
        for t in [*range(1, n_col), 0]:
            if t or o:
                piece_copy(t, o).wait()
            piece += (arecv[t, o] if t or o else asend[0, me]).astype(jnp.float32)
        out[0, g // n_half, lax.rem(g, n_half)] = (piece * scale).astype(jnp.bfloat16)


def body(vecs, poles, weights, kept, roots, order):
    n_row, n_col, n_half = (lax.axis_size(a) for a in ("row", "col", "half"))
    nrows, cols = vecs.shape[1:]
    panel = order.shape[0]
    share, groups, width = panel // n_col, n_row * n_half, panel // n_row
    depth = nrows // groups
    slab = min(SLAB, cols)
    dma = pltpu.SemaphoreType.DMA
    return pl.pallas_call(
        functools.partial(kernel, (n_row, n_col, n_half, cols, panel, slab)),
        out_shape=pltpu.VMEM((1, n_row, n_half, depth, share), jnp.bfloat16),
        in_specs=[pl.BlockSpec(memory_space=pl.ANY)] * 6,
        out_specs=pl.BlockSpec(memory_space=pltpu.VMEM),
        scratch_shapes=[
            pltpu.VMEM((cols // LANES, nrows, LANES), jnp.bfloat16),
            pltpu.VMEM((n_row, 1, width), jnp.float32),
            pltpu.VMEM((panel, LANES), jnp.float32),
            pltpu.VMEM((1, cols), jnp.float32),
            pltpu.VMEM((1, panel), jnp.int32),
            pltpu.VMEM((1, cols), jnp.float32),
            pltpu.VMEM((1, cols), jnp.int32),
            pltpu.VMEM((1, cols), jnp.float32),
            pltpu.VMEM((1, width), jnp.float32),
            pltpu.VMEM((slab // LANES, share, LANES), jnp.bfloat16),
            pltpu.VMEM((nrows, share), jnp.float32),
            pltpu.VMEM((width, LANES), jnp.float32),
            pltpu.VMEM((n_col, groups, depth, share), jnp.bfloat16),
            pltpu.VMEM((n_col, groups, depth, share), jnp.bfloat16),
            pltpu.VMEM((1, width), jnp.float32),
            pltpu.VMEM((n_col, n_half, 1, width), jnp.float32),
            pltpu.VMEM((1, width), jnp.float32),
            pltpu.VMEM((n_row, 1, width), jnp.float32),
            dma((5,)),
            dma((cols // slab,)),
            dma((n_row, n_half)),
            dma((n_row,)),
            dma((n_col, n_half)),
            dma((n_col, n_half)),
            dma((n_row,)),
            dma((n_row,)),
            dma((n_col, groups)),
            dma((n_col, groups)),
        ],
        compiler_params=pltpu.CompilerParams(collective_id=0, has_side_effects=True),
        name="merge",
    )(vecs, poles, weights, kept, roots[None, :], order[None, :])


def solution(mesh):
    return jax.shard_map(
        body,
        mesh=mesh,
        in_specs=(
            P(("grp", "half"), "row", "col"),
            P(("grp", "half"), "col"),
            P(("grp", "half"), "col"),
            P(("grp", "half"), "col"),
            P(("grp", "row")),
            P("grp"),
        ),
        out_specs=P(("grp", "row", "half"), None, None, None, "col"),
        check_vma=False,
    )
```

```python
import functools

import jax
import jax.numpy as jnp
from jax import lax
from jax.experimental import pallas as pl
from jax.experimental.pallas import tpu as pltpu
from jax.sharding import PartitionSpec as P

MESH = pl.DeviceIdType.MESH
LANES = 128
PAIRED = 1
SLAB = 8192


def kernel(dims, vecs, poles, weights, kept, roots, order, out,
           vbuf, rootbuf, theta, scaled, picks, raw, mask, centers, own, acc, nacc, asend, arecv,
           nsend, nrecv, fsend, frecv,
           ssem, vsem, rsend, rrecv, nssem, nrsem, fssem, frsem, assem, arsem):
    n_row, n_col, n_half, cols, panel, slab = dims
    grp, row, col, half = (lax.axis_index(a) for a in ("grp", "row", "col", "half"))
    share = panel // n_col
    width = panel // n_row
    nrows = vbuf.shape[1]
    groups = n_row * n_half
    depth = nrows // groups
    n_slabs = cols // slab
    tiles = slab // LANES
    me = row * n_half + half

    barrier = pltpu.get_barrier_semaphore()
    for o in range(1, groups):
        g = lax.rem(me + o, groups)
        pl.semaphore_signal(barrier, inc=1, device_id=(grp, g // n_half, col, lax.rem(g, n_half)), device_id_type=MESH)
    for t in range(1, n_col):
        for h in range(n_half):
            pl.semaphore_signal(barrier, inc=1, device_id=(grp, row, lax.rem(col + t, n_col), h), device_id_type=MESH)

    small = [(roots, own), (weights, raw), (kept, mask), (poles, centers), (order, picks)]
    fetches = [pltpu.make_async_copy(src, dst, ssem.at[n]) for n, (src, dst) in enumerate(small)]
    for fetch in fetches:
        fetch.start()

    def fetch_tile(n, carry):
        at = pl.ds(pl.multiple_of(n * LANES, LANES), LANES)
        pltpu.make_async_copy(vecs.at[0, :, at], vbuf.at[n], vsem.at[n // tiles]).start()
        return carry

    def loaded(i):
        here = vbuf.at[pl.ds(i * tiles, tiles)]
        pltpu.make_async_copy(here, here, vsem.at[i]).wait()

    lax.fori_loop(0, n_slabs * tiles, fetch_tile, 0)
    pl.semaphore_wait(barrier, groups - 1 + (n_col - 1) * n_half)

    def root_copy(o, h):
        return pltpu.make_async_remote_copy(
            src_ref=roots, dst_ref=rootbuf.at[o], send_sem=rsend.at[o, h], recv_sem=rrecv.at[o],
            device_id=(grp, lax.rem(row + o, n_row), col, h), device_id_type=MESH)

    @pl.when(half == n_half - 1)
    def _():
        for o in range(1, n_row):
            for h in range(n_half):
                root_copy(o, h).start()

    for fetch in fetches:
        fetch.wait()
    scaled[...] = raw[...] * mask[...].astype(jnp.float32)
    nacc[...] = jnp.zeros_like(nacc)
    span = min(width, 128)

    for first in range(0, width, span):
        mine = [jnp.transpose(jnp.broadcast_to(own[:, first:first + span], (LANES, span)))[r:r + 8] for r in range(0, span, 8)]

        def norm_step(i, squares):
            for j in range(4):
                at = pl.ds(pl.multiple_of(i * 4 * LANES + j * LANES, LANES), LANES)
                weight, center = scaled[:, at], centers[:, at]
                cauchy = [weight / (center - m) for m in mine]
                squares = [s + c * c for s, c in zip(squares, cauchy)]
            return squares

        squares = lax.fori_loop(0, cols // (4 * LANES), norm_step, [jnp.zeros((8, LANES), jnp.float32) for _ in mine])
        for n, s in enumerate(squares):
            nacc[pl.ds(first + n * 8, 8), :] = s
    nsend[...] = jnp.sum(jnp.transpose(nacc[...]), axis=0, keepdims=True)

    def norm_copy(t, o):
        return pltpu.make_async_remote_copy(
            src_ref=nsend, dst_ref=nrecv.at[t, o], send_sem=nssem.at[t, o], recv_sem=nrsem.at[t, o],
            device_id=(grp, row, lax.rem(col + t, n_col), lax.rem(half + o, n_half)), device_id_type=MESH)

    norm_copies = [(t, o) for t in range(n_col) for o in range(n_half) if t or o]
    for t, o in norm_copies:
        norm_copy(t, o).start()

    wanted = jnp.transpose(jnp.broadcast_to(picks[...], (LANES, panel)))[:, :width]
    lane = lax.broadcasted_iota(jnp.int32, (panel, width), 1)
    picked = jnp.zeros((panel, width), jnp.float32)
    for o in range(n_row):
        if o:
            root_copy(o, 0).wait_recv()
        source = lax.rem(row + n_row - o, n_row)
        picked = jnp.where(wanted - source * width == lane, rootbuf[o] if o else own[...], picked)
    theta[...] = jnp.broadcast_to(jnp.sum(picked, axis=1, keepdims=True), (panel, LANES))

    def piece_copy(t, o):
        g = lax.rem(me + o, groups)
        return pltpu.make_async_remote_copy(
            src_ref=asend.at[t, g], dst_ref=arecv.at[t, o], send_sem=assem.at[t, o], recv_sem=arsem.at[t, o],
            device_id=(grp, g // n_half, lax.rem(col + t, n_col), lax.rem(g, n_half)), device_id_type=MESH)

    def flush(t):
        asend[t] = acc[...].reshape(groups, depth, share).astype(jnp.bfloat16)
        for o in range(0 if t else 1, groups):
            piece_copy(t, o).start()

    def columns(i, js, thetas):
        ats = [pl.ds(pl.multiple_of(i * slab + j * LANES, LANES), LANES) for j in js]
        rows = [[] for _ in js]
        for n in range(0, share // 16, 2):
            for at, parts in zip(ats, rows):
                weight, center = scaled[:, at], centers[:, at]
                a, b = (center - th for th in thetas[n:n + 2])
                if (n // 2) % 4 < PAIRED:
                    both = weight / (a * b)
                    left, right = both * b, both * a
                else:
                    left, right = weight / a, weight / b
                parts += [left.astype(jnp.bfloat16), right.astype(jnp.bfloat16)]
        return jnp.concatenate([jnp.concatenate(parts, axis=0) for parts in rows], axis=1)

    direct = False

    def chunk(t, *accs):
        base = lax.rem(col + t, n_col) * share

        def step(i, sums):
            if t == 1 or n_col == 1:
                loaded(i)
            thetas = [theta[pl.ds(pl.multiple_of(base + r, 16), 16), :] for r in range(0, share, 16)]
            both = [None, None]
            for m in range(tiles // 2):
                left = jnp.concatenate([vbuf[i * tiles + j] for j in (2 * m, 2 * m + 1)], axis=1)
                right = columns(i, (2 * m, 2 * m + 1), thetas)
                if direct:
                    pltpu.matmul_push_rhs(right, m // 2 % 2, m % 2, transpose=True)
                    pltpu.matmul_acc_lhs(accs[m % 2], left, load_staged_rhs=m // 2 % 2)
                else:
                    part = lax.dot_general(left, right, (((1,), (1,)), ((), ())), preferred_element_type=jnp.float32)
                    both[m % 2] = part if both[m % 2] is None else both[m % 2] + part
            acc[...] += both[0] + both[1]
            return sums

        acc[...] = jnp.zeros_like(acc)
        lax.fori_loop(0, n_slabs, step, 0)

    def run(t):
        if direct:
            pl.run_scoped(functools.partial(chunk, t), *(pltpu.ACC(n)((nrows, share), jnp.float32) for n in range(2)))
        else:
            chunk(t)

    for t in [*range(1, n_col), 0]:
        run(t)
        flush(t)
        if t == 1 or n_col == 1:
            total = nsend[...]
            for pair in norm_copies:
                norm_copy(*pair).wait()
                total += nrecv[pair]
            fsend[...] = lax.rsqrt(total + 1e-06)

            def factor_copy(o):
                return pltpu.make_async_remote_copy(
                    src_ref=fsend, dst_ref=frecv.at[o], send_sem=fssem.at[o], recv_sem=frsem.at[o],
                    device_id=(grp, lax.rem(row + o, n_row), col, half), device_id_type=MESH)

            for o in range(1, n_row):
                factor_copy(o).start()

    chosen = picks[:, pl.ds(pl.multiple_of(col * share, LANES), share)]
    index = lax.broadcasted_iota(jnp.int32, (width, share), 0)
    scale = jnp.zeros((width, share), jnp.float32)
    for o in range(n_row):
        if o:
            factor_copy(o).wait()
        source = lax.rem(row + n_row - o, n_row)
        factor = frecv[o] if o else fsend[...]
        column = jnp.transpose(jnp.broadcast_to(factor, (LANES, width)))[:, :1]
        scale = jnp.where(chosen - source * width == index, column, scale)
    scale = jnp.sum(scale, axis=0, keepdims=True)

    @pl.when(half == n_half - 1)
    def _():
        for o in range(1, n_row):
            for h in range(n_half):
                root_copy(o, h).wait_send()

    for o in range(groups):
        g = lax.rem(me + groups - o, groups)
        piece = jnp.zeros((depth, share), jnp.float32)
        for t in [*range(1, n_col), 0]:
            if t or o:
                piece_copy(t, o).wait()
            piece += (arecv[t, o] if t or o else asend[0, me]).astype(jnp.float32)
        out[0, g // n_half, lax.rem(g, n_half)] = (piece * scale).astype(jnp.bfloat16)


def body(vecs, poles, weights, kept, roots, order):
    n_row, n_col, n_half = (lax.axis_size(a) for a in ("row", "col", "half"))
    nrows, cols = vecs.shape[1:]
    panel = order.shape[0]
    share, groups, width = panel // n_col, n_row * n_half, panel // n_row
    depth = nrows // groups
    slab = min(SLAB, cols)
    dma = pltpu.SemaphoreType.DMA
    return pl.pallas_call(
        functools.partial(kernel, (n_row, n_col, n_half, cols, panel, slab)),
        out_shape=pltpu.VMEM((1, n_row, n_half, depth, share), jnp.bfloat16),
        in_specs=[pl.BlockSpec(memory_space=pl.ANY)] * 6,
        out_specs=pl.BlockSpec(memory_space=pltpu.VMEM),
        scratch_shapes=[
            pltpu.VMEM((cols // LANES, nrows, LANES), jnp.bfloat16),
            pltpu.VMEM((n_row, 1, width), jnp.float32),
            pltpu.VMEM((panel, LANES), jnp.float32),
            pltpu.VMEM((1, cols), jnp.float32),
            pltpu.VMEM((1, panel), jnp.int32),
            pltpu.VMEM((1, cols), jnp.float32),
            pltpu.VMEM((1, cols), jnp.int32),
            pltpu.VMEM((1, cols), jnp.float32),
            pltpu.VMEM((1, width), jnp.float32),
            pltpu.VMEM((nrows, share), jnp.float32),
            pltpu.VMEM((width, LANES), jnp.float32),
            pltpu.VMEM((n_col, groups, depth, share), jnp.bfloat16),
            pltpu.VMEM((n_col, groups, depth, share), jnp.bfloat16),
            pltpu.VMEM((1, width), jnp.float32),
            pltpu.VMEM((n_col, n_half, 1, width), jnp.float32),
            pltpu.VMEM((1, width), jnp.float32),
            pltpu.VMEM((n_row, 1, width), jnp.float32),
            dma((5,)),
            dma((cols // slab,)),
            dma((n_row, n_half)),
            dma((n_row,)),
            dma((n_col, n_half)),
            dma((n_col, n_half)),
            dma((n_row,)),
            dma((n_row,)),
            dma((n_col, groups)),
            dma((n_col, groups)),
        ],
        compiler_params=pltpu.CompilerParams(collective_id=0, has_side_effects=True),
        name="merge",
    )(vecs, poles, weights, kept, roots[None, :], order[None, :])


def solution(mesh):
    return jax.shard_map(
        body,
        mesh=mesh,
        in_specs=(
            P(("grp", "half"), "row", "col"),
            P(("grp", "half"), "col"),
            P(("grp", "half"), "col"),
            P(("grp", "half"), "col"),
            P(("grp", "row")),
            P("grp"),
        ),
        out_specs=P(("grp", "row", "half"), None, None, None, "col"),
        check_vma=False,
    )
```

```python
import functools

import jax
import jax.numpy as jnp
from jax import lax
from jax.experimental import pallas as pl
from jax.experimental.pallas import tpu as pltpu
from jax.sharding import PartitionSpec as P

MESH = pl.DeviceIdType.MESH
LANES = 128
PAIRED = 1
SLAB = 16384


def kernel(dims, vecs, poles, weights, kept, roots, order, out,
           vbuf, rootbuf, theta, scaled, picks, raw, mask, centers, own, acc, nacc, asend, arecv,
           nsend, nrecv, fsend, frecv,
           ssem, vsem, rsend, rrecv, nssem, nrsem, fssem, frsem, assem, arsem):
    n_row, n_col, n_half, cols, panel, slab = dims
    grp, row, col, half = (lax.axis_index(a) for a in ("grp", "row", "col", "half"))
    share = panel // n_col
    width = panel // n_row
    nrows = vbuf.shape[1]
    groups = n_row * n_half
    depth = nrows // groups
    n_slabs = cols // slab
    tiles = slab // LANES
    me = row * n_half + half

    barrier = pltpu.get_barrier_semaphore()
    for o in range(1, groups):
        g = lax.rem(me + o, groups)
        pl.semaphore_signal(barrier, inc=1, device_id=(grp, g // n_half, col, lax.rem(g, n_half)), device_id_type=MESH)
    for t in range(1, n_col):
        for h in range(n_half):
            pl.semaphore_signal(barrier, inc=1, device_id=(grp, row, lax.rem(col + t, n_col), h), device_id_type=MESH)

    small = [(roots, own), (weights, raw), (kept, mask), (poles, centers), (order, picks)]
    fetches = [pltpu.make_async_copy(src, dst, ssem.at[n]) for n, (src, dst) in enumerate(small)]
    for fetch in fetches:
        fetch.start()

    def fetch_tile(n, carry):
        at = pl.ds(pl.multiple_of(n * LANES, LANES), LANES)
        pltpu.make_async_copy(vecs.at[0, :, at], vbuf.at[n], vsem.at[n // tiles]).start()
        return carry

    def loaded(i):
        here = vbuf.at[pl.ds(i * tiles, tiles)]
        pltpu.make_async_copy(here, here, vsem.at[i]).wait()

    lax.fori_loop(0, n_slabs * tiles, fetch_tile, 0)
    pl.semaphore_wait(barrier, groups - 1 + (n_col - 1) * n_half)

    def root_copy(o, h):
        return pltpu.make_async_remote_copy(
            src_ref=roots, dst_ref=rootbuf.at[o], send_sem=rsend.at[o, h], recv_sem=rrecv.at[o],
            device_id=(grp, lax.rem(row + o, n_row), col, h), device_id_type=MESH)

    @pl.when(half == n_half - 1)
    def _():
        for o in range(n_row - 1, 0, -1):
            for h in range(n_half):
                root_copy(o, h).start()

    for fetch in fetches:
        fetch.wait()
    scaled[...] = raw[...] * mask[...].astype(jnp.float32)
    nacc[...] = jnp.zeros_like(nacc)
    span = min(width, 128)

    for first in range(0, width, span):
        mine = [jnp.transpose(jnp.broadcast_to(own[:, first:first + span], (LANES, span)))[r:r + 8] for r in range(0, span, 8)]

        def norm_step(i, squares):
            for j in range(4):
                at = pl.ds(pl.multiple_of(i * 4 * LANES + j * LANES, LANES), LANES)
                weight, center = scaled[:, at], centers[:, at]
                cauchy = [weight / (center - m) for m in mine]
                squares = [s + c * c for s, c in zip(squares, cauchy)]
            return squares

        squares = lax.fori_loop(0, cols // (4 * LANES), norm_step, [jnp.zeros((8, LANES), jnp.float32) for _ in mine])
        for n, s in enumerate(squares):
            nacc[pl.ds(first + n * 8, 8), :] = s
    nsend[...] = jnp.sum(jnp.transpose(nacc[...]), axis=0, keepdims=True)

    def norm_copy(t, o):
        return pltpu.make_async_remote_copy(
            src_ref=nsend, dst_ref=nrecv.at[t, o], send_sem=nssem.at[t, o], recv_sem=nrsem.at[t, o],
            device_id=(grp, row, lax.rem(col + t, n_col), lax.rem(half + o, n_half)), device_id_type=MESH)

    norm_copies = [(t, o) for t in range(n_col) for o in range(n_half) if t or o]
    for t, o in norm_copies:
        norm_copy(t, o).start()

    wanted = jnp.transpose(jnp.broadcast_to(picks[...], (LANES, panel)))[:, :width]
    lane = lax.broadcasted_iota(jnp.int32, (panel, width), 1)
    picked = jnp.zeros((panel, width), jnp.float32)
    for o in range(n_row):
        if o:
            root_copy(o, 0).wait_recv()
        source = lax.rem(row + n_row - o, n_row)
        picked = jnp.where(wanted - source * width == lane, rootbuf[o] if o else own[...], picked)
    theta[...] = jnp.broadcast_to(jnp.sum(picked, axis=1, keepdims=True), (panel, LANES))

    def piece_copy(t, o):
        g = lax.rem(me + o, groups)
        return pltpu.make_async_remote_copy(
            src_ref=asend.at[t, g], dst_ref=arecv.at[t, o], send_sem=assem.at[t, o], recv_sem=arsem.at[t, o],
            device_id=(grp, g // n_half, lax.rem(col + t, n_col), lax.rem(g, n_half)), device_id_type=MESH)

    def flush(t):
        asend[t] = acc[...].reshape(groups, depth, share).astype(jnp.bfloat16)

        for o in range(1, groups):
            piece_copy(t, o).start()

        @pl.when(t > 0)
        def _():
            piece_copy(t, 0).start()

    def columns(i, js, thetas):
        ats = [pl.ds(pl.multiple_of(i * slab + j * LANES, LANES), LANES) for j in js]
        rows = [[] for _ in js]
        for n in range(0, share // 16, 2):
            for at, parts in zip(ats, rows):
                weight, center = scaled[:, at], centers[:, at]
                a, b = (center - th for th in thetas[n:n + 2])
                if (n // 2) % 4 < PAIRED:
                    both = weight / (a * b)
                    left, right = both * b, both * a
                else:
                    left, right = weight / a, weight / b
                parts += [left.astype(jnp.bfloat16), right.astype(jnp.bfloat16)]
        return jnp.concatenate([jnp.concatenate(parts, axis=0) for parts in rows], axis=1)

    def factor_copy(o):
        return pltpu.make_async_remote_copy(
            src_ref=fsend, dst_ref=frecv.at[o], send_sem=fssem.at[o], recv_sem=frsem.at[o],
            device_id=(grp, lax.rem(row + o, n_row), col, half), device_id_type=MESH)

    def chunk(c, carry):
        t = lax.rem(c + 1, n_col)
        base = lax.rem(col + t, n_col) * share
        def step(i, carry):
            @pl.when(c == 0)
            def _():
                loaded(i)

            thetas = [theta[pl.ds(pl.multiple_of(base + r, 16), 16), :] for r in range(0, share, 16)]
            sums = [None, None]
            for m in range(tiles // 2):
                left = jnp.concatenate([vbuf[i * tiles + j] for j in (2 * m, 2 * m + 1)], axis=1)
                right = columns(i, (2 * m, 2 * m + 1), thetas)
                part = lax.dot_general(left, right, (((1,), (1,)), ((), ())), preferred_element_type=jnp.float32)
                sums[m % 2] = part if sums[m % 2] is None else sums[m % 2] + part
            if n_slabs == 1:
                acc[...] = sums[0] + sums[1]
            else:
                acc[...] = jnp.where(i == 0, 0.0, acc[...]) + sums[0] + sums[1]
            return carry

        lax.fori_loop(0, n_slabs, step, 0)
        flush(t)

        @pl.when(c == 0)
        def _():
            total = nsend[...]
            for pair in norm_copies:
                norm_copy(*pair).wait()
                total += nrecv[pair]
            fsend[...] = lax.rsqrt(total + 1e-06)
            for o in range(1, n_row):
                factor_copy(o).start()

        return carry

    lax.fori_loop(0, n_col, chunk, 0)

    chosen = picks[:, pl.ds(pl.multiple_of(col * share, LANES), share)]
    index = lax.broadcasted_iota(jnp.int32, (width, share), 0)
    scale = jnp.zeros((width, share), jnp.float32)
    for o in range(n_row):
        if o:
            factor_copy(o).wait()
        source = lax.rem(row + n_row - o, n_row)
        factor = frecv[o] if o else fsend[...]
        column = jnp.transpose(jnp.broadcast_to(factor, (LANES, width)))[:, :1]
        scale = jnp.where(chosen - source * width == index, column, scale)
    scale = jnp.sum(scale, axis=0, keepdims=True)

    @pl.when(half == n_half - 1)
    def _():
        for o in range(1, n_row):
            for h in range(n_half):
                root_copy(o, h).wait_send()

    for o in range(groups):
        g = lax.rem(me + groups - o, groups)
        piece = jnp.zeros((depth, share), jnp.float32)
        for t in [*range(1, n_col), 0]:
            if t or o:
                piece_copy(t, o).wait()
            piece += (arecv[t, o] if t or o else asend[0, me]).astype(jnp.float32)
        out[0, g // n_half, lax.rem(g, n_half)] = (piece * scale).astype(jnp.bfloat16)


def body(vecs, poles, weights, kept, roots, order):
    n_row, n_col, n_half = (lax.axis_size(a) for a in ("row", "col", "half"))
    nrows, cols = vecs.shape[1:]
    panel = order.shape[0]
    share, groups, width = panel // n_col, n_row * n_half, panel // n_row
    depth = nrows // groups
    slab = min(SLAB, cols)
    dma = pltpu.SemaphoreType.DMA
    return pl.pallas_call(
        functools.partial(kernel, (n_row, n_col, n_half, cols, panel, slab)),
        out_shape=pltpu.VMEM((1, n_row, n_half, depth, share), jnp.bfloat16),
        in_specs=[pl.BlockSpec(memory_space=pl.ANY)] * 6,
        out_specs=pl.BlockSpec(memory_space=pltpu.VMEM),
        scratch_shapes=[
            pltpu.VMEM((cols // LANES, nrows, LANES), jnp.bfloat16),
            pltpu.VMEM((n_row, 1, width), jnp.float32),
            pltpu.VMEM((panel, LANES), jnp.float32),
            pltpu.VMEM((1, cols), jnp.float32),
            pltpu.VMEM((1, panel), jnp.int32),
            pltpu.VMEM((1, cols), jnp.float32),
            pltpu.VMEM((1, cols), jnp.int32),
            pltpu.VMEM((1, cols), jnp.float32),
            pltpu.VMEM((1, width), jnp.float32),
            pltpu.VMEM((nrows, share), jnp.float32),
            pltpu.VMEM((width, LANES), jnp.float32),
            pltpu.VMEM((n_col, groups, depth, share), jnp.bfloat16),
            pltpu.VMEM((n_col, groups, depth, share), jnp.bfloat16),
            pltpu.VMEM((1, width), jnp.float32),
            pltpu.VMEM((n_col, n_half, 1, width), jnp.float32),
            pltpu.VMEM((1, width), jnp.float32),
            pltpu.VMEM((n_row, 1, width), jnp.float32),
            dma((5,)),
            dma((cols // slab,)),
            dma((n_row, n_half)),
            dma((n_row,)),
            dma((n_col, n_half)),
            dma((n_col, n_half)),
            dma((n_row,)),
            dma((n_row,)),
            dma((n_col, groups)),
            dma((n_col, groups)),
        ],
        compiler_params=pltpu.CompilerParams(collective_id=0, has_side_effects=True),
        name="merge",
    )(vecs, poles, weights, kept, roots[None, :], order[None, :])


def solution(mesh):
    return jax.shard_map(
        body,
        mesh=mesh,
        in_specs=(
            P(("grp", "half"), "row", "col"),
            P(("grp", "half"), "col"),
            P(("grp", "half"), "col"),
            P(("grp", "half"), "col"),
            P(("grp", "row")),
            P("grp"),
        ),
        out_specs=P(("grp", "row", "half"), None, None, None, "col"),
        check_vma=False,
    )
```

```python
import functools

import jax
import jax.numpy as jnp
from jax import lax
from jax.experimental import pallas as pl
from jax.experimental.pallas import tpu as pltpu
from jax.sharding import PartitionSpec as P

MESH = pl.DeviceIdType.MESH
LANES = 128
PAIRED = 1
SLAB = 16384


def kernel(dims, vecs, poles, weights, kept, roots, order, out,
           vbuf, rootbuf, theta, scaled, picks, raw, mask, centers, own, acc, nacc, asend, arecv,
           nsend, nrecv, fsend, frecv,
           ssem, vsem, rsend, rrecv, nssem, nrsem, fssem, frsem, assem, arsem):
    n_row, n_col, n_half, cols, panel, slab = dims
    grp, row, col, half = (lax.axis_index(a) for a in ("grp", "row", "col", "half"))
    share = panel // n_col
    width = panel // n_row
    nrows = vbuf.shape[1]
    groups = n_row * n_half
    depth = nrows // groups
    n_slabs = cols // slab
    tiles = slab // LANES
    me = row * n_half + half

    barrier = pltpu.get_barrier_semaphore()
    for o in range(1, groups):
        g = lax.rem(me + o, groups)
        pl.semaphore_signal(barrier, inc=1, device_id=(grp, g // n_half, col, lax.rem(g, n_half)), device_id_type=MESH)
    for t in range(1, n_col):
        for h in range(n_half):
            pl.semaphore_signal(barrier, inc=1, device_id=(grp, row, lax.rem(col + t, n_col), h), device_id_type=MESH)

    small = [(roots, own), (weights, raw), (kept, mask), (poles, centers), (order, picks)]
    fetches = [pltpu.make_async_copy(src, dst, ssem.at[n]) for n, (src, dst) in enumerate(small)]
    for fetch in fetches:
        fetch.start()

    def fetch_tile(n, carry):
        at = pl.ds(pl.multiple_of(n * LANES, LANES), LANES)
        pltpu.make_async_copy(vecs.at[0, :, at], vbuf.at[n], vsem.at[n // tiles]).start()
        return carry

    def loaded(i):
        here = vbuf.at[pl.ds(i * tiles, tiles)]
        pltpu.make_async_copy(here, here, vsem.at[i]).wait()

    lax.fori_loop(0, n_slabs * tiles, fetch_tile, 0)
    pl.semaphore_wait(barrier, groups - 1 + (n_col - 1) * n_half)

    def root_copy(o, h):
        return pltpu.make_async_remote_copy(
            src_ref=roots, dst_ref=rootbuf.at[o], send_sem=rsend.at[o, h], recv_sem=rrecv.at[o],
            device_id=(grp, lax.rem(row + o, n_row), col, h), device_id_type=MESH)

    @pl.when(half == n_half - 1)
    def _():
        for o in range(n_row - 1, 0, -1):
            for h in range(n_half):
                root_copy(o, h).start()

    for fetch in fetches:
        fetch.wait()
    scaled[...] = raw[...] * mask[...].astype(jnp.float32)
    nacc[...] = jnp.zeros_like(nacc)
    span = min(width, 128)

    for first in range(0, width, span):
        mine = [jnp.transpose(jnp.broadcast_to(own[:, first:first + span], (LANES, span)))[r:r + 8] for r in range(0, span, 8)]

        def norm_step(i, squares):
            for j in range(4):
                at = pl.ds(pl.multiple_of(i * 4 * LANES + j * LANES, LANES), LANES)
                weight, center = scaled[:, at], centers[:, at]
                cauchy = [weight / (center - m) for m in mine]
                squares = [s + c * c for s, c in zip(squares, cauchy)]
            return squares

        squares = lax.fori_loop(0, cols // (4 * LANES), norm_step, [jnp.zeros((8, LANES), jnp.float32) for _ in mine])
        for n, s in enumerate(squares):
            nacc[pl.ds(first + n * 8, 8), :] = s
    nsend[...] = jnp.sum(jnp.transpose(nacc[...]), axis=0, keepdims=True)

    def norm_copy(t, o):
        return pltpu.make_async_remote_copy(
            src_ref=nsend, dst_ref=nrecv.at[t, o], send_sem=nssem.at[t, o], recv_sem=nrsem.at[t, o],
            device_id=(grp, row, lax.rem(col + t, n_col), lax.rem(half + o, n_half)), device_id_type=MESH)

    norm_copies = [(t, o) for t in range(n_col) for o in range(n_half) if t or o]
    for t, o in norm_copies:
        norm_copy(t, o).start()

    wanted = jnp.transpose(jnp.broadcast_to(picks[...], (LANES, panel)))[:, :width]
    lane = lax.broadcasted_iota(jnp.int32, (panel, width), 1)
    picked = jnp.zeros((panel, width), jnp.float32)
    for o in range(n_row):
        if o:
            root_copy(o, 0).wait_recv()
        source = lax.rem(row + n_row - o, n_row)
        picked = jnp.where(wanted - source * width == lane, rootbuf[o] if o else own[...], picked)
    theta[...] = jnp.broadcast_to(jnp.sum(picked, axis=1, keepdims=True), (panel, LANES))

    def piece_copy(t, o):
        g = lax.rem(me + o, groups)
        return pltpu.make_async_remote_copy(
            src_ref=asend.at[t, g], dst_ref=arecv.at[t, o], send_sem=assem.at[t, o], recv_sem=arsem.at[t, o],
            device_id=(grp, g // n_half, lax.rem(col + t, n_col), lax.rem(g, n_half)), device_id_type=MESH)

    def flush(t):
        asend[t] = acc[...].reshape(groups, depth, share).astype(jnp.bfloat16)

        for o in range(1, groups):
            piece_copy(t, o).start()

        @pl.when(t > 0)
        def _():
            piece_copy(t, 0).start()

    def columns(i, js, thetas):
        ats = [pl.ds(pl.multiple_of(i * slab + j * LANES, LANES), LANES) for j in js]
        rows = [[] for _ in js]
        for n in range(0, share // 16, 2):
            for at, parts in zip(ats, rows):
                weight, center = scaled[:, at], centers[:, at]
                a, b = (center - th for th in thetas[n:n + 2])
                if (n // 2) % 4 < PAIRED:
                    both = weight / (a * b)
                    left, right = both * b, both * a
                else:
                    left, right = weight / a, weight / b
                parts += [left.astype(jnp.bfloat16), right.astype(jnp.bfloat16)]
        return jnp.concatenate([jnp.concatenate(parts, axis=0) for parts in rows], axis=1)

    def factor_copy(o):
        return pltpu.make_async_remote_copy(
            src_ref=fsend, dst_ref=frecv.at[o], send_sem=fssem.at[o], recv_sem=frsem.at[o],
            device_id=(grp, lax.rem(row + o, n_row), col, half), device_id_type=MESH)

    def chunk(c, carry):
        t = lax.rem(c + n_col - col, n_col)
        base = lax.rem(col + t, n_col) * share
        def step(i, carry):
            @pl.when(c == 0)
            def _():
                loaded(i)

            thetas = [theta[pl.ds(pl.multiple_of(base + r, 16), 16), :] for r in range(0, share, 16)]
            sums = [None, None]
            for m in range(tiles // 2):
                left = jnp.concatenate([vbuf[i * tiles + j] for j in (2 * m, 2 * m + 1)], axis=1)
                right = columns(i, (2 * m, 2 * m + 1), thetas)
                part = lax.dot_general(left, right, (((1,), (1,)), ((), ())), preferred_element_type=jnp.float32)
                sums[m % 2] = part if sums[m % 2] is None else sums[m % 2] + part
            if n_slabs == 1:
                acc[...] = sums[0] + sums[1]
            else:
                acc[...] = jnp.where(i == 0, 0.0, acc[...]) + sums[0] + sums[1]
            return carry

        lax.fori_loop(0, n_slabs, step, 0)
        flush(t)

        @pl.when(c == 0)
        def _():
            total = nsend[...]
            for pair in norm_copies:
                norm_copy(*pair).wait()
                total += nrecv[pair]
            fsend[...] = lax.rsqrt(total + 1e-06)
            for o in range(1, n_row):
                factor_copy(o).start()

        return carry

    lax.fori_loop(0, n_col, chunk, 0)

    chosen = picks[:, pl.ds(pl.multiple_of(col * share, LANES), share)]
    index = lax.broadcasted_iota(jnp.int32, (width, share), 0)
    scale = jnp.zeros((width, share), jnp.float32)
    for o in range(n_row):
        if o:
            factor_copy(o).wait()
        source = lax.rem(row + n_row - o, n_row)
        factor = frecv[o] if o else fsend[...]
        column = jnp.transpose(jnp.broadcast_to(factor, (LANES, width)))[:, :1]
        scale = jnp.where(chosen - source * width == index, column, scale)
    scale = jnp.sum(scale, axis=0, keepdims=True)

    @pl.when(half == n_half - 1)
    def _():
        for o in range(1, n_row):
            for h in range(n_half):
                root_copy(o, h).wait_send()

    for o in range(groups):
        g = lax.rem(me + groups - o, groups)
        piece = jnp.zeros((depth, share), jnp.float32)
        for t in [*range(1, n_col), 0]:
            if t or o:
                piece_copy(t, o).wait()
            piece += (arecv[t, o] if t or o else asend[0, me]).astype(jnp.float32)
        out[0, g // n_half, lax.rem(g, n_half)] = (piece * scale).astype(jnp.bfloat16)


def body(vecs, poles, weights, kept, roots, order):
    n_row, n_col, n_half = (lax.axis_size(a) for a in ("row", "col", "half"))
    nrows, cols = vecs.shape[1:]
    panel = order.shape[0]
    share, groups, width = panel // n_col, n_row * n_half, panel // n_row
    depth = nrows // groups
    slab = min(SLAB, cols)
    dma = pltpu.SemaphoreType.DMA
    return pl.pallas_call(
        functools.partial(kernel, (n_row, n_col, n_half, cols, panel, slab)),
        out_shape=pltpu.VMEM((1, n_row, n_half, depth, share), jnp.bfloat16),
        in_specs=[pl.BlockSpec(memory_space=pl.ANY)] * 6,
        out_specs=pl.BlockSpec(memory_space=pltpu.VMEM),
        scratch_shapes=[
            pltpu.VMEM((cols // LANES, nrows, LANES), jnp.bfloat16),
            pltpu.VMEM((n_row, 1, width), jnp.float32),
            pltpu.VMEM((panel, LANES), jnp.float32),
            pltpu.VMEM((1, cols), jnp.float32),
            pltpu.VMEM((1, panel), jnp.int32),
            pltpu.VMEM((1, cols), jnp.float32),
            pltpu.VMEM((1, cols), jnp.int32),
            pltpu.VMEM((1, cols), jnp.float32),
            pltpu.VMEM((1, width), jnp.float32),
            pltpu.VMEM((nrows, share), jnp.float32),
            pltpu.VMEM((width, LANES), jnp.float32),
            pltpu.VMEM((n_col, groups, depth, share), jnp.bfloat16),
            pltpu.VMEM((n_col, groups, depth, share), jnp.bfloat16),
            pltpu.VMEM((1, width), jnp.float32),
            pltpu.VMEM((n_col, n_half, 1, width), jnp.float32),
            pltpu.VMEM((1, width), jnp.float32),
            pltpu.VMEM((n_row, 1, width), jnp.float32),
            dma((5,)),
            dma((cols // slab,)),
            dma((n_row, n_half)),
            dma((n_row,)),
            dma((n_col, n_half)),
            dma((n_col, n_half)),
            dma((n_row,)),
            dma((n_row,)),
            dma((n_col, groups)),
            dma((n_col, groups)),
        ],
        compiler_params=pltpu.CompilerParams(collective_id=0, has_side_effects=True),
        name="merge",
    )(vecs, poles, weights, kept, roots[None, :], order[None, :])


def solution(mesh):
    return jax.shard_map(
        body,
        mesh=mesh,
        in_specs=(
            P(("grp", "half"), "row", "col"),
            P(("grp", "half"), "col"),
            P(("grp", "half"), "col"),
            P(("grp", "half"), "col"),
            P(("grp", "row")),
            P("grp"),
        ),
        out_specs=P(("grp", "row", "half"), None, None, None, "col"),
        check_vma=False,
    )
```

```python
import functools

import jax
import jax.numpy as jnp
from jax import lax
from jax.experimental import pallas as pl
from jax.experimental.pallas import tpu as pltpu
from jax.sharding import PartitionSpec as P

MESH = pl.DeviceIdType.MESH
LANES = 128
PAIRED = 1
SLAB = 16384


def kernel(dims, vecs, poles, weights, kept, roots, order, out,
           vbuf, rootbuf, theta, scaled, picks, raw, mask, centers, own, acc, nacc, asend, arecv,
           nsend, nrecv, fsend, frecv,
           ssem, vsem, rsend, rrecv, nssem, nrsem, fssem, frsem, assem, arsem):
    n_row, n_col, n_half, cols, panel, slab = dims
    grp, row, col, half = (lax.axis_index(a) for a in ("grp", "row", "col", "half"))
    share = panel // n_col
    width = panel // n_row
    nrows = vbuf.shape[1]
    groups = n_row * n_half
    depth = nrows // groups
    n_slabs = cols // slab
    tiles = slab // LANES
    me = row * n_half + half

    barrier = pltpu.get_barrier_semaphore()
    for o in range(1, groups):
        g = lax.rem(me + o, groups)
        pl.semaphore_signal(barrier, inc=1, device_id=(grp, g // n_half, col, lax.rem(g, n_half)), device_id_type=MESH)
    for t in range(1, n_col):
        for h in range(n_half):
            pl.semaphore_signal(barrier, inc=1, device_id=(grp, row, lax.rem(col + t, n_col), h), device_id_type=MESH)

    small = [(roots, own), (weights, raw), (kept, mask), (poles, centers), (order, picks)]
    fetches = [pltpu.make_async_copy(src, dst, ssem.at[n]) for n, (src, dst) in enumerate(small)]
    for fetch in fetches:
        fetch.start()

    def fetch_tile(n, carry):
        at = pl.ds(pl.multiple_of(n * LANES, LANES), LANES)
        pltpu.make_async_copy(vecs.at[0, :, at], vbuf.at[n], vsem.at[n // tiles]).start()
        return carry

    def loaded(i):
        here = vbuf.at[pl.ds(i * tiles, tiles)]
        pltpu.make_async_copy(here, here, vsem.at[i]).wait()

    lax.fori_loop(0, n_slabs * tiles, fetch_tile, 0)
    pl.semaphore_wait(barrier, groups - 1 + (n_col - 1) * n_half)

    def root_copy(o, h):
        return pltpu.make_async_remote_copy(
            src_ref=roots, dst_ref=rootbuf.at[o], send_sem=rsend.at[o, h], recv_sem=rrecv.at[o],
            device_id=(grp, lax.rem(row + o, n_row), col, h), device_id_type=MESH)

    @pl.when(half == n_half - 1)
    def _():
        for o in range(n_row - 1, 0, -1):
            for h in range(n_half):
                root_copy(o, h).start()

    for fetch in fetches:
        fetch.wait()
    scaled[...] = raw[...] * mask[...].astype(jnp.float32)
    nacc[...] = jnp.zeros_like(nacc)
    span = min(width, 128)

    for first in range(0, width, span):
        mine = [jnp.transpose(jnp.broadcast_to(own[:, first:first + span], (LANES, span)))[r:r + 8] for r in range(0, span, 8)]

        def norm_step(i, squares):
            for j in range(4):
                at = pl.ds(pl.multiple_of(i * 4 * LANES + j * LANES, LANES), LANES)
                weight, center = scaled[:, at], centers[:, at]
                cauchy = [weight / (center - m) for m in mine]
                squares = [s + c * c for s, c in zip(squares, cauchy)]
            return squares

        squares = lax.fori_loop(0, cols // (4 * LANES), norm_step, [jnp.zeros((8, LANES), jnp.float32) for _ in mine])
        for n, s in enumerate(squares):
            nacc[pl.ds(first + n * 8, 8), :] = s
    nsend[...] = jnp.sum(jnp.transpose(nacc[...]), axis=0, keepdims=True)

    def norm_copy(t, o):
        return pltpu.make_async_remote_copy(
            src_ref=nsend, dst_ref=nrecv.at[t, o], send_sem=nssem.at[t, o], recv_sem=nrsem.at[t, o],
            device_id=(grp, row, lax.rem(col + t, n_col), lax.rem(half + o, n_half)), device_id_type=MESH)

    norm_copies = [(t, o) for t in range(n_col) for o in range(n_half) if t or o]
    for t, o in norm_copies:
        norm_copy(t, o).start()

    wanted = jnp.transpose(jnp.broadcast_to(picks[...], (LANES, panel)))[:, :width]
    lane = lax.broadcasted_iota(jnp.int32, (panel, width), 1)
    picked = jnp.zeros((panel, width), jnp.float32)
    for o in range(n_row):
        if o:
            root_copy(o, 0).wait_recv()
        source = lax.rem(row + n_row - o, n_row)
        picked = jnp.where(wanted - source * width == lane, rootbuf[o] if o else own[...], picked)
    theta[...] = jnp.broadcast_to(jnp.sum(picked, axis=1, keepdims=True), (panel, LANES))

    def piece_copy(t, o):
        g = lax.rem(me + o, groups)
        return pltpu.make_async_remote_copy(
            src_ref=asend.at[t, g], dst_ref=arecv.at[t, o], send_sem=assem.at[t, o], recv_sem=arsem.at[t, o],
            device_id=(grp, g // n_half, lax.rem(col + t, n_col), lax.rem(g, n_half)), device_id_type=MESH)

    def flush(t):
        asend[t] = acc[...].reshape(groups, depth, share).astype(jnp.bfloat16)

        for o in range(1, groups):
            piece_copy(t, o).start()

        @pl.when(t > 0)
        def _():
            piece_copy(t, 0).start()

    def columns(i, js, thetas):
        ats = [pl.ds(pl.multiple_of(i * slab + j * LANES, LANES), LANES) for j in js]
        rows = [[] for _ in js]
        for n in range(0, share // 16, 2):
            for at, parts in zip(ats, rows):
                weight, center = scaled[:, at], centers[:, at]
                a, b = (center - th for th in thetas[n:n + 2])
                if (n // 2) % 4 < PAIRED:
                    both = weight / (a * b)
                    left, right = both * b, both * a
                else:
                    left, right = weight / a, weight / b
                parts += [left.astype(jnp.bfloat16), right.astype(jnp.bfloat16)]
        return jnp.concatenate([jnp.concatenate(parts, axis=0) for parts in rows], axis=1)

    def factor_copy(o):
        return pltpu.make_async_remote_copy(
            src_ref=fsend, dst_ref=frecv.at[o], send_sem=fssem.at[o], recv_sem=frsem.at[o],
            device_id=(grp, lax.rem(row + o, n_row), col, half), device_id_type=MESH)

    def chunk(c, carry):
        t = lax.rem(c + n_col - col, n_col)
        base = lax.rem(col + t, n_col) * share
        def step(i, carry):
            @pl.when(c == 0)
            def _():
                loaded(i)

            thetas = [theta[pl.ds(pl.multiple_of(base + r, 16), 16), :] for r in range(0, share, 16)]
            sums = [None, None]
            for m in range(tiles // 2):
                left = jnp.concatenate([vbuf[i * tiles + j] for j in (2 * m, 2 * m + 1)], axis=1)
                right = columns(i, (2 * m, 2 * m + 1), thetas)
                part = lax.dot_general(left, right, (((1,), (1,)), ((), ())), preferred_element_type=jnp.float32)
                sums[m % 2] = part if sums[m % 2] is None else sums[m % 2] + part
            if n_slabs == 1:
                acc[...] = sums[0] + sums[1]
            else:
                acc[...] = jnp.where(i == 0, 0.0, acc[...]) + sums[0] + sums[1]
            return carry

        lax.fori_loop(0, n_slabs, step, 0)
        flush(t)

        @pl.when(c == 0)
        def _():
            total = nsend[...]
            for pair in norm_copies:
                norm_copy(*pair).wait()
                total += nrecv[pair]
            fsend[...] = lax.rsqrt(total + 1e-06)
            for o in range(1, n_row):
                factor_copy(o).start()

        return carry

    lax.fori_loop(0, n_col, chunk, 0)

    chosen = picks[:, pl.ds(pl.multiple_of(col * share, LANES), share)]
    index = lax.broadcasted_iota(jnp.int32, (width, share), 0)
    scale = jnp.zeros((width, share), jnp.float32)
    for o in range(n_row):
        if o:
            factor_copy(o).wait()
        source = lax.rem(row + n_row - o, n_row)
        factor = frecv[o] if o else fsend[...]
        column = jnp.transpose(jnp.broadcast_to(factor, (LANES, width)))[:, :1]
        scale = jnp.where(chosen - source * width == index, column, scale)
    scale = jnp.sum(scale, axis=0, keepdims=True)

    @pl.when(half == n_half - 1)
    def _():
        for o in range(1, n_row):
            for h in range(n_half):
                root_copy(o, h).wait_send()

    for o in range(groups - 1, -1, -1):
        g = lax.rem(me + groups - o, groups)
        piece = jnp.zeros((depth, share), jnp.float32)
        for t in [*range(1, n_col), 0]:
            if t or o:
                piece_copy(t, o).wait()
            piece += (arecv[t, o] if t or o else asend[0, me]).astype(jnp.float32)
        out[0, g // n_half, lax.rem(g, n_half)] = (piece * scale).astype(jnp.bfloat16)


def body(vecs, poles, weights, kept, roots, order):
    n_row, n_col, n_half = (lax.axis_size(a) for a in ("row", "col", "half"))
    nrows, cols = vecs.shape[1:]
    panel = order.shape[0]
    share, groups, width = panel // n_col, n_row * n_half, panel // n_row
    depth = nrows // groups
    slab = min(SLAB, cols)
    dma = pltpu.SemaphoreType.DMA
    return pl.pallas_call(
        functools.partial(kernel, (n_row, n_col, n_half, cols, panel, slab)),
        out_shape=pltpu.VMEM((1, n_row, n_half, depth, share), jnp.bfloat16),
        in_specs=[pl.BlockSpec(memory_space=pl.ANY)] * 6,
        out_specs=pl.BlockSpec(memory_space=pltpu.VMEM),
        scratch_shapes=[
            pltpu.VMEM((cols // LANES, nrows, LANES), jnp.bfloat16),
            pltpu.VMEM((n_row, 1, width), jnp.float32),
            pltpu.VMEM((panel, LANES), jnp.float32),
            pltpu.VMEM((1, cols), jnp.float32),
            pltpu.VMEM((1, panel), jnp.int32),
            pltpu.VMEM((1, cols), jnp.float32),
            pltpu.VMEM((1, cols), jnp.int32),
            pltpu.VMEM((1, cols), jnp.float32),
            pltpu.VMEM((1, width), jnp.float32),
            pltpu.VMEM((nrows, share), jnp.float32),
            pltpu.VMEM((width, LANES), jnp.float32),
            pltpu.VMEM((n_col, groups, depth, share), jnp.bfloat16),
            pltpu.VMEM((n_col, groups, depth, share), jnp.bfloat16),
            pltpu.VMEM((1, width), jnp.float32),
            pltpu.VMEM((n_col, n_half, 1, width), jnp.float32),
            pltpu.VMEM((1, width), jnp.float32),
            pltpu.VMEM((n_row, 1, width), jnp.float32),
            dma((5,)),
            dma((cols // slab,)),
            dma((n_row, n_half)),
            dma((n_row,)),
            dma((n_col, n_half)),
            dma((n_col, n_half)),
            dma((n_row,)),
            dma((n_row,)),
            dma((n_col, groups)),
            dma((n_col, groups)),
        ],
        compiler_params=pltpu.CompilerParams(collective_id=0, has_side_effects=True),
        name="merge",
    )(vecs, poles, weights, kept, roots[None, :], order[None, :])


def solution(mesh):
    return jax.shard_map(
        body,
        mesh=mesh,
        in_specs=(
            P(("grp", "half"), "row", "col"),
            P(("grp", "half"), "col"),
            P(("grp", "half"), "col"),
            P(("grp", "half"), "col"),
            P(("grp", "row")),
            P("grp"),
        ),
        out_specs=P(("grp", "row", "half"), None, None, None, "col"),
        check_vma=False,
    )
```
